256 devices in a mesh: row: 16 (over x_lo, y, core), col: 16 (over z, x_hi).
Axes of the slice: x: 4 (x_hi: 2, x_lo: 2; x = x_hi * 2 + x_lo), y: 4, z: 8, core: 2. Of those that a mesh axis runs over, the one named last changes fastest.
Arguments:
- adj_values: bfloat16 [2, 16, 16, 20, 128, 128], P(None, 'row', 'col'), may hold values from -6 to 6
- block_rows: int32 [2, 16, 16, 20], P(None, 'row', 'col'), may hold values from 0 to 47, as said below
- block_cols: int32 [2, 16, 16, 20], P(None, 'row', 'col'), may hold values from 0 to 15, as said below
- block_counts: int32 [2, 16, 16], P(None, 'row', 'col'), may hold values from 5 to 20, as said below
- block_scales: bfloat16 [2, 16, 16, 20], P(None, 'row', 'col'), may hold values from 0.0049743652 to 0.049804688
- panel_features: bfloat16 [2, 256, 32768], P(None, 'col', 'row'), may hold values from -6 to 6
- weight: bfloat16 [256, 256], replicated, may hold values from -0.375 to 0.375
- out_bias: float32 [256], replicated, may hold values from -3 to 3
Outputs:
- layer_out: bfloat16 [98304, 256], P(('row', 'col'))
The draws below stay inside these ranges and needn't reach their ends.
Inputs may be any that keep to these rules, and one draw needn't show every extreme that they name: `block_rows`: block rows are local to the 48 block rows of a row index. The slots of one device in one panel name distinct (block row, block column) pairs. `block_cols`: block columns index the 16 block columns of a col index's part of the panel. `block_counts`: in every panel, all devices of at least one row index hold exactly 20 live blocks.
All inputs are finite; a program needn't handle non-finite values.
Results may differ from the reference program's by a relative error of at most 0.0044.
Values may be sent and summed in bfloat16 or wider, within the bound.
No kernel may reach another device: no remote copies, remote signals or barrier semaphores. Data moves between devices by JAX's collectives and lax.ppermute only.
A program may use at most 64 MiB of HBM per device.

```python
import math
import jax
import jax.numpy as jnp
from jax import lax

F = 256
BS = 128
ROWB_DEV = 48
PCB = 16
STEPS = 2
MAXB = 20
PANEL = 32768
N_ROW = 16
N_COL = 16


def cell_order(key):
    cell_total = ROWB_DEV * PCB
    shape = (STEPS, N_ROW, N_COL, cell_total)
    noise = jax.random.randint(jax.random.fold_in(key, 11), shape, 0, 4096)
    heavy_rows = jax.random.randint(jax.random.fold_in(key, 12), (STEPS, N_ROW, N_COL, 1), 0, ROWB_DEV)
    cell_ids = jnp.arange(cell_total, dtype=jnp.int32)
    distance = jnp.abs(cell_ids // PCB - heavy_rows)
    scores = (noise + 64 * distance) * cell_total + cell_ids
    ranked = jnp.argsort(scores, axis=-1).astype(jnp.int32)
    return ranked[..., :MAXB]


def draw_block_rows(key, part):
    return (cell_order(key) // PCB).astype(jnp.int32)


def draw_block_cols(key, part):
    return (cell_order(key) % PCB).astype(jnp.int32)


def draw_block_counts(key, part):
    base = jax.random.randint(jax.random.fold_in(key, 21), (STEPS, N_ROW, N_COL), MAXB // 4, MAXB // 2 + 1)
    full_row = jax.random.randint(jax.random.fold_in(key, 22), (STEPS, 1, 1), 0, N_ROW)
    row_ids = jnp.arange(N_ROW, dtype=jnp.int32)[None, :, None]
    return jnp.where(row_ids == full_row, MAXB, base).astype(jnp.int32)


def block_levels(own_key, shape, shards, smallest, largest):
    loudness = 1.0
    for dim, shards_of in shards:
        steps = jax.random.uniform(jax.random.fold_in(jax.random.fold_in(own_key, 6), dim), (shards_of,), jnp.float32, smallest / len(shards), largest / len(shards))
        loudness = loudness * jnp.repeat(jnp.exp(steps), shape[dim] // shards_of).reshape((-1,) + (1,) * (len(shape) - 1 - dim))
    return loudness


def bell_draw(key, shape, scale, most, split=(), held_as=jnp.bfloat16):
    loudness = block_levels(key, shape, split, -0.22, 0.18) if split else 1.0
    values = jax.random.normal(key, shape, jnp.float32) * scale * loudness
    return jnp.minimum(jnp.maximum(values, -most), most).astype(held_as)


def setup_inputs(seed: int = 0) -> dict:
    keys = jax.random.split(jax.random.key(seed), 9)
    adj_values = bell_draw(keys[0], (STEPS, N_ROW, N_COL, MAXB, BS, BS), 1.0, 6.0, ((1, 16), (2, 16)))
    block_rows = draw_block_rows(jax.random.fold_in(keys[8], 71), 0)
    block_cols = draw_block_cols(jax.random.fold_in(keys[8], 71), 0)
    block_counts = draw_block_counts(jax.random.fold_in(keys[8], 71), 0)
    block_scales = jnp.clip(jnp.exp(math.log(0.049804688) - 2.3038113 * jax.random.uniform(keys[4], (STEPS, N_ROW, N_COL, MAXB), jnp.float32) ** block_levels(keys[4], (STEPS, N_ROW, N_COL, MAXB), ((1, 16), (2, 16)), -0.2, 0.2)), 0.0049743652, 0.049804688).astype(jnp.bfloat16)
    panel_features = bell_draw(keys[5], (STEPS, F, PANEL), 1.0, 6.0, ((1, 16), (2, 16)))
    weight = bell_draw(keys[6], (F, F), F ** -0.5, 0.375)
    out_bias = bell_draw(keys[7], (F,), 0.5, 3.0, (), jnp.float32)
    return dict(adj_values=adj_values, block_rows=block_rows, block_cols=block_cols, block_counts=block_counts, block_scales=block_scales, panel_features=panel_features, weight=weight, out_bias=out_bias)


def row_group(hblocks, values, row_ids, col_ids, counts, scales):
    col_total = row_ids.shape[0]
    slot_total = row_ids.shape[1]
    owners = jnp.arange(col_total, dtype=jnp.int32)[:, None]
    global_cols = (owners * PCB + col_ids).reshape(-1).astype(jnp.int32)
    live_mask = jnp.arange(slot_total, dtype=jnp.int32)[None, :] < counts[:, None]
    live_scale = jnp.where(live_mask, scales.astype(jnp.float32), jnp.float32(0.0)).reshape(-1)
    feature_cols = hblocks[global_cols].astype(jnp.float32)
    flattened = values.reshape(col_total * slot_total, BS, BS).astype(jnp.float32)
    contrib = jnp.einsum("bfk,brk->bfr", feature_cols, flattened, precision=lax.Precision.HIGHEST)
    contrib = contrib * live_scale[:, None, None]
    return jax.ops.segment_sum(contrib, row_ids.reshape(-1).astype(jnp.int32), num_segments=ROWB_DEV)


def reference(adj_values, block_rows, block_cols, block_counts, block_scales, panel_features, weight, out_bias):
    running = jnp.zeros((N_ROW, ROWB_DEV, F, BS), jnp.float32)
    for step in range(STEPS):
        hblocks = panel_features[step].reshape(F, PCB * N_COL, BS).transpose(1, 0, 2)

        def one_group(gathered):
            return row_group(hblocks, gathered[0], gathered[1], gathered[2], gathered[3], gathered[4])

        running = running + lax.map(one_group, (adj_values[step], block_rows[step], block_cols[step], block_counts[step], block_scales[step]))
    aggregate = running.astype(jnp.bfloat16)
    before = jnp.einsum("nzfr,fg->nzrg", aggregate.astype(jnp.float32), weight.astype(jnp.float32), precision=lax.Precision.HIGHEST)
    before = before.reshape(N_ROW * ROWB_DEV * BS, F)
    return jax.nn.relu(before + out_bias).astype(jnp.bfloat16)
```

```python
import jax
import jax.numpy as jnp
from jax import lax
from jax.experimental import pallas as pl
from jax.experimental.pallas import tpu as pltpu
from jax.sharding import Mesh
from jax.sharding import PartitionSpec as P

ROWS = 48
BS = 128
MAXB = 20
STEPS = 2
NZ = 8
HALF = 128
GROUP = 4
ROW = ("xl", "y", "core")
COL = ("z", "xh")
SWAP = [(0, 1), (1, 0)]


def shift(n, by):
    return [(i, (i + by) % n) for i in range(n)]


def shift_and_cross(by):
    return [(z * 2 + h, (z + by) % NZ * 2 + 1 - h) for z in range(NZ) for h in range(2)]


def to_plane(k):
    pairs = []
    for xl in range(2):
        for y in range(4):
            for z in range(NZ):
                source_xl = xl if z // 4 == k else 1 - xl
                pairs.append(((xl * 4 + y) * NZ + z, (xl * 4 + z % 4) * NZ + source_xl * 4 + y))
    return pairs


def block_kernel(own, par, feats0, feats1, adj_own, adj_par, part, fwd, bwd, cross):
    core, xl = lax.axis_index("core"), lax.axis_index("xl")
    z, xh = lax.axis_index("z"), lax.axis_index("xh")
    flip = jnp.where(xl == z // 4, 0, 1)
    part[...] = jnp.zeros_like(part)

    def run(feats, adj, table):
        for t in range(STEPS):
            live = table[6 + t, 0].astype(jnp.int32)

            def group(g, carry):
                prods = []
                for u in range(GROUP):
                    slot = g * GROUP + u
                    at = pl.ds(pl.multiple_of(table[2 + t, slot].astype(jnp.int32) * BS, BS), BS)
                    x = jnp.concatenate([feats[p ^ flip, t, :, at] for p in range(8)], axis=0)
                    prods.append(
                        lax.dot_general(
                            adj[t * MAXB + slot], x, (((1,), (1,)), ((), ())), preferred_element_type=jnp.float32
                        )
                    )
                for u in range(GROUP):
                    slot = g * GROUP + u
                    row = table[t, slot].astype(jnp.int32)
                    stop = (row // 6 - z) & (NZ - 1)
                    place = stop * 6 + (((row // 3) & 1) ^ xh) * 3 + row % 3
                    scale = jnp.where(slot < live, table[4 + t, slot], 0.0)
                    part[place] = part[place] + prods[u] * scale
                return carry

            lax.fori_loop(0, (live + GROUP - 1) // GROUP, group, 0)

    @pl.when(core == xh)
    def _():
        run(feats0, adj_own, own)
        run(feats1, adj_par, par)

    @pl.when(core != xh)
    def _():
        run(feats1, adj_own, own)
        run(feats0, adj_par, par)

    for i, place in enumerate((24, 21)):
        fwd[i] = part[pl.ds(place, 3)].astype(fwd.dtype)
    for i, place in enumerate((27, 30)):
        bwd[i] = part[pl.ds(place, 3)].astype(bwd.dtype)
    cross[...] = part[pl.ds(3, 3)].astype(cross.dtype)


def block_products(own, par, feats0, feats1, adj_own, adj_par):
    smem = pl.BlockSpec(memory_space=pltpu.SMEM)
    vmem = pl.BlockSpec(memory_space=pltpu.VMEM)
    message = jax.ShapeDtypeStruct((2, 3, BS, HALF), jnp.bfloat16)
    return pl.pallas_call(
        block_kernel,
        out_shape=(
            jax.ShapeDtypeStruct((ROWS, BS, HALF), jnp.float32),
            message,
            message,
            jax.ShapeDtypeStruct((3, BS, HALF), jnp.bfloat16),
        ),
        in_specs=[smem, smem, vmem, vmem, vmem, vmem],
        out_specs=(vmem, vmem, vmem, vmem),
        cost_estimate=pl.CostEstimate(flops=80 * 2 * BS**3, bytes_accessed=9 << 20, transcendentals=0),
        name="block_products",
    )(own, par, feats0, feats1, adj_own, adj_par)


def body(adj_values, block_rows, block_cols, block_counts, block_scales, features, weight, out_bias):
    y = lax.axis_index("y")
    z, xh = (lax.axis_index(a) for a in COL)
    swapped = lax.ppermute(features, "xl", SWAP)
    adj = adj_values.reshape(STEPS * MAXB, BS, BS)
    adj_par = lax.ppermute(adj, "xh", SWAP)
    slots = (STEPS, MAXB)
    table = jnp.concatenate(
        [
            block_rows.reshape(slots).astype(jnp.float32),
            block_cols.reshape(slots).astype(jnp.float32),
            block_scales.reshape(slots).astype(jnp.float32),
            jnp.broadcast_to(block_counts.reshape(STEPS, 1), slots).astype(jnp.float32),
        ]
    )
    table_par = lax.ppermute(table, "xh", SWAP)

    low_plane = z < 4
    first = lax.ppermute(jnp.where(low_plane, features, swapped), ("xl", "y", "z"), to_plane(0))
    second = lax.ppermute(jnp.where(low_plane, swapped, features), ("xl", "y", "z"), to_plane(1))
    here = jnp.stack([first, second])
    below = lax.ppermute(here, "y", shift(4, 1))
    above = lax.ppermute(here, "y", shift(4, -1))
    far0 = lax.ppermute(below[:1], "y", shift(4, 1))
    far1 = lax.ppermute(above[1:], "y", shift(4, -1))
    feats0 = jnp.concatenate([here, below, above, far0, far1])
    feats1 = lax.ppermute(feats0, "core", SWAP)

    part, fwd, bwd, cross = block_products(table, table_par, feats0, feats1, adj, adj_par)
    part = part.reshape(NZ, 2, 3, BS, HALF)

    def low(v):
        return v.astype(jnp.bfloat16)

    def full(v):
        return v.astype(jnp.float32)

    ahead, back = shift(NZ, 1), shift(NZ, -1)
    got_f = full(lax.ppermute(fwd, "z", ahead))
    got_b = full(lax.ppermute(bwd, "z", back))
    crossed = full(lax.ppermute(cross, "xh", SWAP))
    fwd = low(got_f + jnp.stack([part[3, 0], part[2, 1]]))
    bwd = low(got_b + jnp.stack([part[5, 1], part[6, 0]]))
    got_f = full(lax.ppermute(fwd, "z", ahead))
    got_b = full(lax.ppermute(bwd, "z", back))
    fwd = low(got_f[0] + part[2, 0])
    fwd_cross = low(got_f[1] + part[1, 1])
    bwd = low(got_b + jnp.stack([part[6, 1], part[7, 0]]))
    got_f = full(lax.ppermute(fwd, "z", ahead))
    got_b = full(lax.ppermute(bwd, "z", back))
    crossed_f = full(lax.ppermute(fwd_cross, COL, shift_and_cross(1)))
    last_f = full(lax.ppermute(low(got_f + part[1, 0]), "z", ahead))
    crossed_b = full(lax.ppermute(low(got_b[0] + part[7, 1]), COL, shift_and_cross(-1)))
    mine = low(part[0, 0] + last_f + got_b[1])
    other = low(crossed + crossed_f + crossed_b)

    w = weight.reshape(2, 4, 2, 16, 256)
    w = jnp.concatenate([w, w], axis=1)
    w = lax.dynamic_slice_in_dim(w, y, 4, axis=1)
    w = jnp.stack([w[:, i] for i in (0, 3, 1, 2)])
    w_mine = jnp.where(xh == 0, w[:, :, 0], w[:, :, 1]).reshape(HALF, 256)
    w_other = jnp.where(xh == 0, w[:, :, 1], w[:, :, 0]).reshape(HALF, 256)
    before = jnp.dot(mine.reshape(-1, HALF), w_mine, preferred_element_type=jnp.float32)
    before = before + jnp.dot(other.reshape(-1, HALF), w_other, preferred_element_type=jnp.float32)
    return jax.nn.relu(before + out_bias).astype(jnp.bfloat16)


def solution(mesh):
    split = Mesh(mesh.devices.reshape(2, 4, 2, 8, 2), ROW + COL)
    in_specs = (
        P(None, ROW, COL, None, None, None),
        P(None, ROW, COL, None),
        P(None, ROW, COL, None),
        P(None, ROW, COL),
        P(None, ROW, COL, None),
        P(None, COL, ROW),
        P(),
        P(),
    )
    return jax.shard_map(body, mesh=split, in_specs=in_specs, out_specs=P(ROW + COL, None), check_vma=False)
```

```python
import jax
import jax.numpy as jnp
from jax import lax
from jax.experimental import pallas as pl
from jax.experimental.pallas import tpu as pltpu
from jax.sharding import Mesh
from jax.sharding import PartitionSpec as P

ROWS = 48
BS = 128
MAXB = 20
STEPS = 2
NZ = 8
HALF = 128
GROUP = 4
ROW = ("xl", "y", "core")
COL = ("z", "xh")
SWAP = [(0, 1), (1, 0)]


def shift(n, by):
    return [(i, (i + by) % n) for i in range(n)]


def shift_and_cross(by):
    return [(z * 2 + h, (z + by) % NZ * 2 + 1 - h) for z in range(NZ) for h in range(2)]


def to_plane(k):
    pairs = []
    for xl in range(2):
        for y in range(4):
            for z in range(NZ):
                source_xl = xl if z // 4 == k else 1 - xl
                pairs.append(((xl * 4 + y) * NZ + z, (xl * 4 + z % 4) * NZ + source_xl * 4 + y))
    return pairs


def block_kernel(own, par, feats0, feats1, adj_own, adj_par, keep0, keep2, keep6, msg1, msg3, msg5, msg7, msg4a, msg4b, part):
    core, xl = lax.axis_index("core"), lax.axis_index("xl")
    z, xh = lax.axis_index("z"), lax.axis_index("xh")
    flip = jnp.where(xl == z // 4, 0, 1)
    part[...] = jnp.zeros_like(part)

    def run(feats, adj, table):
        for t in range(STEPS):
            live = table[6 + t, 0].astype(jnp.int32)

            def group(g, carry):
                prods = []
                for u in range(GROUP):
                    slot = g * GROUP + u
                    at = pl.ds(pl.multiple_of(table[2 + t, slot].astype(jnp.int32) * BS, BS), BS)
                    x = jnp.concatenate([feats[p ^ flip, t, :, at] for p in range(8)], axis=0)
                    prods.append(
                        lax.dot_general(
                            adj[t * MAXB + slot], x, (((1,), (1,)), ((), ())), preferred_element_type=jnp.float32
                        )
                    )
                for u in range(GROUP):
                    slot = g * GROUP + u
                    row = table[t, slot].astype(jnp.int32)
                    stop = (row // 6 - z) & (NZ - 1)
                    half = ((row // 3) & 1) ^ xh
                    scale = jnp.where(slot < live, table[4 + t, slot], 0.0)
                    place = stop * 6 + half * 3 + row % 3
                    part[place] = part[place] + prods[u] * scale
                return carry

            lax.fori_loop(0, (live + GROUP - 1) // GROUP, group, 0)

    @pl.when(core == xh)
    def _():
        run(feats0, adj_own, own)
        run(feats1, adj_par, par)

    @pl.when(core != xh)
    def _():
        run(feats1, adj_own, own)
        run(feats0, adj_par, par)

    for ref, stop in ((msg3, 3), (msg5, 5), (msg1, 1), (msg7, 7), (keep2, 2), (keep6, 6), (keep0, 0)):
        for half in range(2):
            ref[half] = part[pl.ds(stop * 6 + half * 3, 3)].astype(ref.dtype)
    for ref, half in ((msg4a, 0), (msg4b, 1)):
        ref[...] = part[pl.ds(24 + half * 3, 3)].astype(ref.dtype)


def block_products(own, par, feats0, feats1, adj_own, adj_par):
    smem = pl.BlockSpec(memory_space=pltpu.SMEM)
    vmem = pl.BlockSpec(memory_space=pltpu.VMEM)
    keep = jax.ShapeDtypeStruct((2, 3, BS, HALF), jnp.float32)
    message = jax.ShapeDtypeStruct((2, 3, BS, HALF), jnp.bfloat16)
    single = jax.ShapeDtypeStruct((3, BS, HALF), jnp.bfloat16)
    return pl.pallas_call(
        block_kernel,
        out_shape=(keep,) * 3 + (message,) * 4 + (single,) * 2,
        in_specs=[smem, smem, vmem, vmem, vmem, vmem],
        out_specs=(vmem,) * 9,
        scratch_shapes=[pltpu.VMEM((ROWS, BS, HALF), jnp.float32)],
        compiler_params=pltpu.CompilerParams(vmem_limit_bytes=16 << 20),
        cost_estimate=pl.CostEstimate(flops=80 * 2 * BS**3, bytes_accessed=9 << 20, transcendentals=0),
        name="block_products",
    )(own, par, feats0, feats1, adj_own, adj_par)


def body(adj_values, block_rows, block_cols, block_counts, block_scales, features, weight, out_bias):
    y = lax.axis_index("y")
    z, xh = (lax.axis_index(a) for a in COL)
    swapped = lax.ppermute(features, "xl", SWAP)
    slots = (STEPS, MAXB)
    table = jnp.concatenate(
        [
            block_rows.reshape(slots).astype(jnp.float32),
            block_cols.reshape(slots).astype(jnp.float32),
            block_scales.reshape(slots).astype(jnp.float32),
            jnp.broadcast_to(block_counts.reshape(STEPS, 1), slots).astype(jnp.float32),
        ]
    )
    table_par = lax.ppermute(table, "xh", SWAP)
    adj = adj_values.reshape(STEPS * MAXB, BS, BS)
    adj_par = lax.ppermute(adj, "xh", SWAP)

    low_plane = z < 4
    first = lax.ppermute(jnp.where(low_plane, features, swapped), ("xl", "y", "z"), to_plane(0))
    second = lax.ppermute(jnp.where(low_plane, swapped, features), ("xl", "y", "z"), to_plane(1))
    here, table, table_par = lax.optimization_barrier((jnp.stack([first, second]), table, table_par))
    below = lax.ppermute(here, "y", shift(4, 1))
    above = lax.ppermute(here, "y", shift(4, -1))
    far0 = lax.ppermute(below[:1], "y", shift(4, 1))
    far1 = lax.ppermute(above[1:], "y", shift(4, -1))
    feats0 = jnp.concatenate([here, below, above, far0, far1])
    feats1 = lax.ppermute(feats0, "core", SWAP)

    keep0, keep2, keep6, msg1, msg3, msg5, msg7, msg4a, msg4b = block_products(
        table, table_par, feats0, feats1, adj, adj_par
    )

    def low(v):
        return v.astype(jnp.bfloat16)

    def full(v):
        return v.astype(jnp.float32)

    def along(v, by):
        return full(lax.ppermute(v, "z", shift(NZ, by)))

    def across(v, by):
        return full(lax.ppermute(v, COL, shift_and_cross(by)))

    got3, got5 = along(msg3, 1), along(msg5, -1)
    got4a, got4b = along(msg4a, 2), along(msg4b, -2)
    got1, got7 = along(msg1, 1), along(msg7, -1)
    ahead_mine = along(low(keep2[0] + got3[0] + got4a), 2)
    back_mine = along(low(keep6[0] + got5[0]), -2)
    ahead_cross = across(low(keep2[1] + got3[1]), 2)
    back_cross = across(low(keep6[1] + got5[1] + got4b), -2)
    near_cross = full(lax.ppermute(low(keep0[1] + got1[1] + got7[1]), "xh", SWAP))
    mine = low(keep0[0] + got1[0] + got7[0] + ahead_mine + back_mine)
    other = low(near_cross + ahead_cross + back_cross)

    w = weight.reshape(2, 4, 2, 16, 256)
    w = jnp.concatenate([w, w], axis=1)
    w = lax.dynamic_slice_in_dim(w, y, 4, axis=1)
    w = jnp.stack([w[:, i] for i in (0, 3, 1, 2)])
    w_mine = jnp.where(xh == 0, w[:, :, 0], w[:, :, 1]).reshape(HALF, 256)
    w_other = jnp.where(xh == 0, w[:, :, 1], w[:, :, 0]).reshape(HALF, 256)
    before = jnp.dot(mine.reshape(-1, HALF), w_mine, preferred_element_type=jnp.float32)
    before = before + jnp.dot(other.reshape(-1, HALF), w_other, preferred_element_type=jnp.float32)
    return jax.nn.relu(before + out_bias).astype(jnp.bfloat16)


def solution(mesh):
    split = Mesh(mesh.devices.reshape(2, 4, 2, 8, 2), ROW + COL)
    in_specs = (
        P(None, ROW, COL, None, None, None),
        P(None, ROW, COL, None),
        P(None, ROW, COL, None),
        P(None, ROW, COL),
        P(None, ROW, COL, None),
        P(None, COL, ROW),
        P(),
        P(),
    )

    return jax.shard_map(body, mesh=split, in_specs=in_specs, out_specs=P(ROW + COL, None), check_vma=False)
```
